32 devices in a mesh: seq: 16 (over z, y, x), head: 2 (over core).
Axes of the slice: x: 2, y: 2, z: 4, core: 2. Of those that a mesh axis runs over, the one named last changes fastest.
Arguments:
- queries: float32 [8192, 4096], P('seq', 'head'), may hold values from -6 to 6
- keys: float32 [8192, 4096], P('seq', 'head'), may hold values from -6 to 6
- values: float32 [8192, 4096], P('seq', 'head'), may hold values from -6 to 6
- log_decay: float32 [32, 8192], P('head', 'seq'), may hold values from -1 to 0, as said below
- level_weights: float32 [32, 14, 8192], P('head', None, 'seq'), may hold values from 0.25 to 2.5
- norm_gain: float32 [4096], P('head'), may hold values from 0.1 to 1.9
- out_weight: float32 [4096, 2048], P('head', 'seq'), may hold values from -0.09375 to 0.09375
Outputs:
- mixed: float32 [8192, 2048], P('seq', 'head')
The draws below stay inside these ranges and needn't reach their ends.
Inputs may be any that keep to these rules, and one draw needn't show every extreme that they name: `log_decay`: every entry is non-positive.
All inputs are finite; a program needn't handle non-finite values.
Results may differ from the reference program's by a relative error of at most 0.0003.
Values sent between devices are 32-bit elements; how exact they have to be, the bound alone decides.
A program may use at most 192 MiB of HBM per device.

```python
import math
import jax
import jax.numpy as jnp
from jax import lax

D = 2048
HEAD_TOTAL = 32
DH = 128
TOK_DEV = 512
HD = 4096
SEQUENCE_TOKENS = 8192
TOK_BITS = 9
SEQ_BITS = 4
LEVELS = 14
N_SEQ = 16


def draw_log_decay(key, part):
    every_key_row = jax.random.split(jax.random.fold_in(key, 7), 5)
    share = 0.5
    fast_heads = jax.random.uniform(every_key_row[0], (HEAD_TOTAL,)) < share
    fast_rate = jnp.log(10.0) / jax.random.uniform(every_key_row[1], (HEAD_TOTAL,), minval=30.0, maxval=50.0)
    slow_rate = jnp.full((HEAD_TOTAL,), 0.3 * jnp.log(10.0) / SEQUENCE_TOKENS, jnp.float32)
    rate_head = jnp.where(fast_heads, fast_rate, slow_rate)
    factor = jnp.exp(jax.random.uniform(every_key_row[2], (HEAD_TOTAL, SEQUENCE_TOKENS), minval=jnp.log(0.5), maxval=jnp.log(2.0)))
    base_offset = -rate_head[:, None] * factor
    group_position = jax.random.randint(every_key_row[3], (HEAD_TOTAL, 2), 0, SEQUENCE_TOKENS)
    group_depth = jax.random.uniform(every_key_row[4], (HEAD_TOTAL, 2), minval=0.22, maxval=0.69)
    match_count = (jnp.arange(SEQUENCE_TOKENS, dtype=jnp.int32)[None, None, :] == group_position[:, :, None]).astype(jnp.float32)
    token_group = -jnp.sum(match_count * group_depth[:, :, None], axis=1)
    return jnp.clip(base_offset + token_group, -1.0, 0.0).astype(jnp.float32)


def block_scale(rng, dims, cuts, smallest, high):
    gain, own = 1.0, jax.random.fold_in(rng, 6)
    for position, blocks in cuts:
        heights = jnp.exp(jax.random.uniform(jax.random.fold_in(own, position), (blocks,), jnp.float32, smallest / len(cuts), high / len(cuts)))
        gain = gain * jnp.repeat(heights, dims[position] // blocks).reshape([-1 if axis == position else 1 for axis in range(len(dims))])
    return gain


def gaussian(key, shape, spread, bound, pieces=(), kind=jnp.bfloat16):
    drawn = jax.random.normal(key, shape, jnp.float32) * spread
    if len(pieces) > 0:
        drawn = block_scale(key, shape, pieces, -0.22, 0.18) * drawn
    return jnp.clip(drawn, min=-bound, max=bound).astype(kind)


def setup_inputs(seed: int = 0) -> dict:
    key_of = jax.random.split(jax.random.key(seed), 8)
    queries = gaussian(key_of[0], (SEQUENCE_TOKENS, HD), 1.0, 6.0, ((0, 16), (1, 2)), jnp.float32)
    keys = gaussian(key_of[1], (SEQUENCE_TOKENS, HD), 1.0, 6.0, ((0, 16), (1, 2)), jnp.float32)
    values = gaussian(key_of[2], (SEQUENCE_TOKENS, HD), 1.0, 6.0, ((0, 16), (1, 2)), jnp.float32)
    log_decay = draw_log_decay(jax.random.fold_in(key_of[7], 71), 0)
    level_weights = jnp.clip(jnp.exp(math.log(2.5) - 2.3025851 * jax.random.uniform(key_of[4], (HEAD_TOTAL, LEVELS, SEQUENCE_TOKENS), jnp.float32) ** block_scale(key_of[4], (HEAD_TOTAL, LEVELS, SEQUENCE_TOKENS), ((0, 2), (2, 16)), -0.2, 0.2)), 0.25, 2.5)
    norm_gain = jnp.clip(1.0 + 0.18 * jax.random.normal(key_of[5], (HD,), jnp.float32), 0.1, 1.9)
    out_weight = gaussian(key_of[6], (HD, D), HD ** -0.5, 0.09375, ((0, 2), (1, 16)), jnp.float32)
    return dict(queries=queries, keys=keys, values=values, log_decay=log_decay, level_weights=level_weights, norm_gain=norm_gain, out_weight=out_weight)


HIGH = lax.Precision.HIGHEST

def level_table(count, bits):
    positions = jnp.arange(count, dtype=jnp.int32)
    mixed_bits = positions[:, None] ^ positions[None, :]
    level_ids = jnp.zeros((count, count), jnp.int32)
    for level_bit in range(bits):
        level_ids = level_ids + (mixed_bits >> level_bit > 0).astype(jnp.int32)
    return level_ids

def reference(queries, keys, values, log_decay, level_weights, norm_gain, out_weight):
    spans = N_SEQ
    tok_count = TOK_DEV
    head_count = HEAD_TOTAL
    head_size = DH
    query_heads = queries.reshape(spans, tok_count, head_count, head_size) * head_size ** (-0.5)
    key_heads = keys.reshape(spans, tok_count, head_count, head_size)
    value_heads = values.reshape(spans, tok_count, head_count, head_size)
    decay_sum = jnp.cumsum(log_decay.reshape(head_count, spans, tok_count), axis=2)
    span_decay = decay_sum[:, :, -1]
    start_decay = jnp.concatenate([jnp.zeros((head_count, 1), jnp.float32), jnp.cumsum(span_decay, axis=1)[:, :-1]], axis=1)
    end_decay = start_decay + span_decay
    fade_weight = jnp.exp(span_decay[:, :, None] - decay_sum)
    span_states = jnp.einsum('cjhd,hcj,cjhe->chde', key_heads, fade_weight, value_heads, precision=HIGH)
    span_ids = jnp.arange(spans, dtype=jnp.int32)
    weight_list = []
    for level_bit in range(SEQ_BITS):
        upper_side = span_ids >> level_bit & 1 == 1
        sibling = span_ids[None, :] >> level_bit == (span_ids[:, None] >> level_bit) - 1
        chosen = upper_side[:, None] & sibling
        gap = jnp.where(chosen[None], start_decay[:, :, None] - end_decay[:, None, :], -jnp.inf)
        weight_list.append(jnp.exp(gap))
    far_mix = jnp.stack(weight_list, axis=0).transpose(2, 0, 1, 3)
    lam_all = level_weights.reshape(head_count, LEVELS, spans, tok_count).transpose(2, 0, 1, 3)
    decay_spans = decay_sum.transpose(1, 0, 2)
    onehot = (level_table(tok_count, TOK_BITS)[None] == jnp.arange(TOK_BITS + 1, dtype=jnp.int32)[:, None, None]).astype(jnp.float32)
    positions = jnp.arange(tok_count, dtype=jnp.int32)
    causal = positions[:, None] >= positions[None, :]

    def one_span(inputs):
        query_c, key_c, value_c, decay_c, lam_c, mix_c = inputs
        near = jnp.einsum('hli,lij->hij', lam_c[:, :TOK_BITS + 1, :], onehot, precision=HIGH)
        gap = jnp.where(causal[None], decay_c[:, :, None] - decay_c[:, None, :], -jnp.inf)
        scores = jnp.einsum('ihd,jhd->hij', query_c, key_c, precision=HIGH) * near * jnp.exp(gap)
        local_out = jnp.einsum('hij,jhd->ihd', scores, value_c, precision=HIGH)
        level_states = jnp.einsum('lhe,ehdf->hldf', mix_c, span_states, precision=HIGH)
        far_weight = lam_c[:, TOK_BITS + 1:, :] * jnp.exp(decay_c)[:, None, :]
        weighted = query_c[:, :, None, :] * far_weight.transpose(2, 0, 1)[:, :, :, None]
        far_out = jnp.einsum('ihld,hlde->ihe', weighted, level_states, precision=HIGH)
        total_out = local_out + far_out
        root_mean = jnp.sqrt(lax.optimization_barrier(jnp.mean(total_out * total_out, axis=-1, keepdims=True)) + 1e-06)
        return (total_out / root_mean).reshape(tok_count, head_count * head_size) * norm_gain
    normed = lax.map(one_span, (query_heads, key_heads, value_heads, decay_spans, lam_all, far_mix))
    normed = normed.reshape(spans * tok_count, head_count * head_size)
    return jnp.dot(normed, out_weight, precision=HIGH, preferred_element_type=jnp.float32)
```

```python
import functools

import jax
import jax.numpy as jnp
from jax import lax
from jax.experimental import pallas as pl
from jax.experimental.pallas import tpu as pltpu
from jax.sharding import PartitionSpec as P

LANES = 128
PAD_ROWS = 8
VMEM_LIMIT = 48 * 1024 * 1024


def split(x):
    high = x.astype(jnp.bfloat16)
    low = (x - high.astype(jnp.float32)).astype(jnp.bfloat16)
    return high, low


def mm(a, b):
    return jnp.dot(a, b, preferred_element_type=jnp.float32)


def dot3(a, b):
    (ah, al), (bh, bl) = split(a), split(b)
    return mm(ah, bh) + (mm(al, bh) + mm(ah, bl))


def params():
    return pltpu.CompilerParams(vmem_limit_bytes=VMEM_LIMIT)


def state_kernel(k_ref, v_ref, c_ref, o_ref):
    c = c_ref[0]
    end = c[:, -1:]
    size = k_ref.shape[1]
    o_ref[0, :size, :] = dot3(v_ref[...].T * jnp.exp(end - c), k_ref[...])
    o_ref[0, size:, :] = jnp.broadcast_to(end, (PAD_ROWS, size))


def near_kernel(base_bits, tok_bits, q_ref, k_ref, v_ref, c_ref, w_ref, o_ref):
    size = q_ref.shape[1]
    base = 1 << base_bits
    tok_count = q_ref.shape[0]
    q_t = (q_ref[...] * size ** (-0.5)).T
    v_t = v_ref[...].T
    rows = lax.broadcasted_iota(jnp.int32, (base, base), 0)
    cols = lax.broadcasted_iota(jnp.int32, (base, base), 1)
    mixed = rows ^ cols
    for block in range(tok_count // base):
        at = slice(block * base, (block + 1) * base)
        c = c_ref[0, :, at]
        column = jnp.broadcast_to(c, (base, base)).T
        weight = jnp.broadcast_to(w_ref[0, 0:1, at], (base, base))
        for bit in range(base_bits):
            weight = jnp.where(mixed >> bit > 0, w_ref[0, bit + 1 : bit + 2, at], weight)
        gap = jnp.where(cols >= rows, c - column, -jnp.inf)
        scores = dot3(k_ref[at, :], q_t[:, at]) * weight * jnp.exp(gap)
        total = dot3(v_t[:, at], scores)
        o_ref[0, :, at] = total
    for bit in range(base_bits, tok_bits):
        span = 1 << bit
        for pair in range(tok_count // (2 * span)):
            low = slice(2 * pair * span, (2 * pair + 1) * span)
            high = slice((2 * pair + 1) * span, (2 * pair + 2) * span)
            c_low, c_high = c_ref[0, :, low], c_ref[0, :, high]
            end = c_low[:, -1:]
            state = dot3(v_t[:, low] * jnp.exp(end - c_low), k_ref[low, :])
            weight = w_ref[0, bit + 1 : bit + 2, high] * jnp.exp(c_high - end)
            o_ref[0, :, high] += dot3(state, q_t[:, high] * weight)


def far_kernel(levels, q_ref, near_ref, w_ref, gain_ref, *refs):
    states, (high_ref, low_ref) = refs[:levels], refs[levels:]
    size = q_ref.shape[1]
    q_t = (q_ref[...] * size ** (-0.5)).T
    total = near_ref[0]
    for level in range(levels):
        total += dot3(states[level][0, :size, :], q_t * w_ref[0, level : level + 1, :])
    mean = jnp.mean(total * total, axis=0, keepdims=True)
    normed = (total / jnp.sqrt(mean + 1e-06)).T * gain_ref[...]
    high, low = split(normed)
    high_ref[...] = high
    low_ref[...] = low


def project_kernel(places_ref, high_ref, low_ref, *refs):
    pieces, out_ref = refs[:5], refs[-1]
    width = pieces[0].shape[1]
    high, low = high_ref[...], low_ref[...]

    def product(left_high, left_low, right):
        right_high, right_low = split(right)
        return mm(left_high, right_high) + (mm(left_low, right_high) + mm(left_high, right_low))

    def put(index, value):
        start = pl.multiple_of(places_ref[1 + index] * width, width)
        out_ref[:, pl.ds(start, width)] = value

    first = jnp.concatenate([pieces[0][...], pieces[1][...]], axis=1)
    result = product(high, low, first)
    put(0, result[:, :width])
    put(1, result[:, width:])
    corner = jnp.concatenate([pieces[3][...], pieces[4][...]], axis=0)
    second = jnp.concatenate([pieces[2][...], corner], axis=1)
    result = product(high, low, second)
    put(2, result[:, :width])
    put(3, result[:, width:])


def plain_kernel(high_ref, low_ref, w_ref, o_ref):
    right_high, right_low = split(w_ref[...])
    high = high_ref[...]
    o_ref[...] = mm(high, right_high) + (mm(low_ref[...], right_high) + mm(high, right_low))


def from_partner(value, mask):
    pairs = [(source, source ^ mask) for source in range(lax.axis_size("seq"))]
    return lax.ppermute(value, "seq", pairs)


def local(queries, keys, values, log_decay, level_weights, norm_gain, out_weight):
    head_count, tok_count = log_decay.shape
    feature_count = queries.shape[1]
    size = feature_count // head_count
    tok_bits = tok_count.bit_length() - 1
    seq_size = lax.axis_size("seq")
    seq_bits = seq_size.bit_length() - 1
    seq_index = lax.axis_index("seq")
    head_size, head_index = lax.axis_size("head"), lax.axis_index("head")
    width = out_weight.shape[1]
    spread = width % LANES == 0 and seq_bits >= 2

    groups = []
    if spread:
        half = feature_count // 2
        for step in range(seq_size // 4):
            own = out_weight if step == 0 else from_partner(out_weight, 4 * step)
            groups.append([own])
        for step, group in enumerate(groups):
            own = group[0]
            by_x, by_y = from_partner(own, 1), from_partner(own, 2)
            corner_low = from_partner(by_x[:half], 2)
            corner_high = from_partner(by_y[half:], 1)
            group += [by_x, by_y, corner_low, corner_high]

    decay_sum = jnp.cumsum(log_decay, axis=1)
    decay_rows = decay_sum[:, None, :]
    tok_spec = pl.BlockSpec((tok_count, size), lambda h: (0, h))
    row_spec = pl.BlockSpec((1, 1, tok_count), lambda h: (h, 0, 0))
    state_spec = pl.BlockSpec((1, size + PAD_ROWS, size), lambda h: (h, 0, 0))
    out_spec = pl.BlockSpec((1, size, tok_count), lambda h: (h, 0, 0))
    state_flops = 6 * feature_count * tok_count * size
    call_state = pl.pallas_call(
        state_kernel,
        grid=(head_count,),
        in_specs=[tok_spec, tok_spec, row_spec],
        out_specs=state_spec,
        out_shape=jax.ShapeDtypeStruct((head_count, size + PAD_ROWS, size), jnp.float32),
        compiler_params=params(),
        cost_estimate=pl.CostEstimate(
            flops=state_flops,
            bytes_accessed=2 * keys.size * 4,
            transcendentals=head_count * tok_count,
        ),
        name="own_state",
    )
    own_state = call_state(keys, values, decay_rows)

    near_levels = level_weights[:, : tok_bits + 1, :]
    base_bits = min(LANES.bit_length() - 1, tok_bits)
    call_near = pl.pallas_call(
        functools.partial(near_kernel, base_bits, tok_bits),
        grid=(head_count,),
        in_specs=[
            tok_spec,
            tok_spec,
            tok_spec,
            row_spec,
            pl.BlockSpec((1, tok_bits + 1, tok_count), lambda h: (h, 0, 0)),
        ],
        out_specs=out_spec,
        out_shape=jax.ShapeDtypeStruct((head_count, size, tok_count), jnp.float32),
        compiler_params=params(),
        cost_estimate=pl.CostEstimate(
            flops=16 * state_flops,
            bytes_accessed=4 * keys.size * 4,
            transcendentals=head_count * tok_count * LANES,
        ),
        name="near",
    )
    near = call_near(queries, keys, values, decay_rows, near_levels)

    block = own_state
    inside = jnp.zeros((head_count,), jnp.float32)
    states, reaches = [], []
    for level_bit in range(seq_bits):
        other = from_partner(block, 2**level_bit)
        is_upper = seq_index >> level_bit & 1 == 1
        states.append(other)
        reaches.append(jnp.where(is_upper, jnp.exp(inside), 0.0))
        other_decay = other[:, size, 0]
        inside = jnp.where(is_upper, inside + other_decay, inside)
        if level_bit < seq_bits - 1:
            mine_decay = block[:, size:, :]
            decay_other = other[:, size:, :]
            late = jnp.where(is_upper, mine_decay, decay_other)[:, :1, :]
            low = jnp.where(is_upper, other, block)[:, :size, :]
            high = jnp.where(is_upper, block, other)[:, :size, :]
            merged = jnp.exp(late) * low + high
            block = jnp.concatenate([merged, mine_decay + decay_other], axis=1)
    far_weight = (
        level_weights[:, tok_bits + 1 :, :]
        * jnp.exp(decay_sum)[:, None, :]
        * jnp.stack(reaches, axis=1)[:, :, None]
    )
    call_far = pl.pallas_call(
        functools.partial(far_kernel, seq_bits),
        grid=(head_count,),
        in_specs=[
            tok_spec,
            out_spec,
            pl.BlockSpec((1, seq_bits, tok_count), lambda h: (h, 0, 0)),
            pl.BlockSpec((1, size), lambda h: (0, h)),
        ]
        + [state_spec] * seq_bits,
        out_specs=[tok_spec, tok_spec],
        out_shape=[jax.ShapeDtypeStruct((tok_count, feature_count), jnp.bfloat16)] * 2,
        compiler_params=params(),
        cost_estimate=pl.CostEstimate(
            flops=seq_bits * state_flops,
            bytes_accessed=3 * keys.size * 4,
            transcendentals=0,
        ),
        name="far",
    )
    normed_high, normed_low = call_far(
        queries, near, far_weight, norm_gain[None, :], *states
    )

    column_count = width * seq_size
    partial_shape = jax.ShapeDtypeStruct((tok_count, column_count), jnp.float32)
    whole = pl.BlockSpec(memory_space=pltpu.VMEM)
    if spread:
        partials = None
        low_bits = seq_index & 3
        for step, group in enumerate(groups):
            places = jnp.stack([(seq_index >> 2) ^ step] + [low_bits ^ e for e in range(4)])
            full = lambda rows, columns: pl.BlockSpec((rows, columns), lambda i, p: (0, 0))
            carried = [] if partials is None else [partials]
            partials = pl.pallas_call(
                project_kernel,
                grid_spec=pltpu.PrefetchScalarGridSpec(
                    num_scalar_prefetch=1,
                    grid=(1,),
                    in_specs=[full(tok_count, feature_count)] * 2
                    + [full(*piece.shape) for piece in group]
                    + [pl.BlockSpec(memory_space=pl.ANY)] * len(carried),
                    out_specs=pl.BlockSpec((tok_count, 4 * width), lambda i, p: (0, p[0])),
                ),
                out_shape=partial_shape,
                input_output_aliases={8: 0} if carried else {},
                compiler_params=params(),
                cost_estimate=pl.CostEstimate(
                    flops=6 * tok_count * feature_count * 4 * width,
                    bytes_accessed=4 * (feature_count * 4 * width + 2 * tok_count * feature_count),
                    transcendentals=0,
                ),
                name="project",
            )(places.astype(jnp.int32), normed_high, normed_low, *group, *carried)
    else:
        gathered = lax.all_gather(out_weight, "seq", axis=1, tiled=True)
        step = min(4 * LANES, column_count)
        partials = pl.pallas_call(
            plain_kernel,
            grid=(column_count // step,),
            in_specs=[
                pl.BlockSpec((tok_count, feature_count), lambda i: (0, 0)),
                pl.BlockSpec((tok_count, feature_count), lambda i: (0, 0)),
                pl.BlockSpec((feature_count, step), lambda i: (0, i)),
            ],
            out_specs=pl.BlockSpec((tok_count, step), lambda i: (0, i)),
            out_shape=partial_shape,
            compiler_params=params(),
            name="project",
        )(normed_high, normed_low, gathered)
    if head_size != 2:
        return lax.psum_scatter(partials, "head", scatter_dimension=1, tiled=True)
    share = column_count // 2
    sent = lax.dynamic_slice(partials, (0, (1 - head_index) * share), (tok_count, share))
    kept = lax.dynamic_slice(partials, (0, head_index * share), (tok_count, share))
    return kept + lax.ppermute(sent, "head", [(0, 1), (1, 0)])


def solution(mesh):
    return jax.shard_map(
        local,
        mesh=mesh,
        in_specs=(
            P("seq", "head"),
            P("seq", "head"),
            P("seq", "head"),
            P("head", "seq"),
            P("head", None, "seq"),
            P("head"),
            P("head", "seq"),
        ),
        out_specs=P("seq", "head"),
        check_vma=False,
    )
```

```python
import functools

import jax
import jax.numpy as jnp
from jax import lax
from jax.experimental import pallas as pl
from jax.experimental.pallas import tpu as pltpu
from jax.sharding import PartitionSpec as P

LANES = 128
PAD_ROWS = 8
VMEM_LIMIT = 48 * 1024 * 1024


def split(x):
    high = x.astype(jnp.bfloat16)
    low = (x - high.astype(jnp.float32)).astype(jnp.bfloat16)
    return high, low


def mm(a, b):
    return jnp.dot(a, b, preferred_element_type=jnp.float32)


def dot3(a, b):
    (ah, al), (bh, bl) = split(a), split(b)
    return mm(ah, bh) + (mm(al, bh) + mm(ah, bl))


def params():
    return pltpu.CompilerParams(vmem_limit_bytes=VMEM_LIMIT)


def state_kernel(k_ref, v_ref, c_ref, o_ref):
    c = c_ref[0]
    end = c[:, -1:]
    size = k_ref.shape[1]
    o_ref[0, :size, :] = dot3(v_ref[...].T * jnp.exp(end - c), k_ref[...])
    o_ref[0, size:, :] = jnp.broadcast_to(end, (PAD_ROWS, size))


def near_kernel(base_bits, tok_bits, q_ref, k_ref, v_ref, c_ref, w_ref, o_ref):
    size = q_ref.shape[1]
    base = 1 << base_bits
    tok_count = q_ref.shape[0]
    q_t = (q_ref[...] * size ** (-0.5)).T
    v_t = v_ref[...].T
    rows = lax.broadcasted_iota(jnp.int32, (base, base), 0)
    cols = lax.broadcasted_iota(jnp.int32, (base, base), 1)
    mixed = rows ^ cols
    for block in range(tok_count // base):
        at = slice(block * base, (block + 1) * base)
        c = c_ref[0, :, at]
        column = jnp.broadcast_to(c, (base, base)).T
        weight = jnp.broadcast_to(w_ref[0, 0:1, at], (base, base))
        for bit in range(base_bits):
            weight = jnp.where(mixed >> bit > 0, w_ref[0, bit + 1 : bit + 2, at], weight)
        gap = jnp.where(cols >= rows, c - column, -jnp.inf)
        scores = dot3(k_ref[at, :], q_t[:, at]) * weight * jnp.exp(gap)
        total = dot3(v_t[:, at], scores)
        o_ref[0, :, at] = total
    for bit in range(base_bits, tok_bits):
        span = 1 << bit
        for pair in range(tok_count // (2 * span)):
            low = slice(2 * pair * span, (2 * pair + 1) * span)
            high = slice((2 * pair + 1) * span, (2 * pair + 2) * span)
            c_low, c_high = c_ref[0, :, low], c_ref[0, :, high]
            end = c_low[:, -1:]
            state = dot3(v_t[:, low] * jnp.exp(end - c_low), k_ref[low, :])
            weight = w_ref[0, bit + 1 : bit + 2, high] * jnp.exp(c_high - end)
            o_ref[0, :, high] += dot3(state, q_t[:, high] * weight)


def far_sum(q_ref, near_ref, w_ref, states):
    size = q_ref.shape[1]
    q_t = (q_ref[...] * size ** (-0.5)).T
    total = near_ref[0]
    for level, state in enumerate(states):
        total += dot3(state[0, :size, :], q_t * w_ref[0, level : level + 1, :])
    return total


def early_kernel(q_ref, near_ref, w_ref, *refs):
    refs[-1][0] = far_sum(q_ref, near_ref, w_ref, refs[:-1])


def far_kernel(q_ref, near_ref, w_ref, gain_ref, *refs):
    states, (high_ref, low_ref) = refs[:-2], refs[-2:]
    total = far_sum(q_ref, near_ref, w_ref, states)
    mean = jnp.mean(total * total, axis=0, keepdims=True)
    normed = (total / jnp.sqrt(mean + 1e-06)).T * gain_ref[...]
    high, low = split(normed)
    high_ref[...] = high
    low_ref[...] = low


def project_kernel(places_ref, high_ref, low_ref, *refs):
    pieces, out_ref = refs[:5], refs[-1]
    width = pieces[0].shape[1]
    high, low = high_ref[...], low_ref[...]

    def product(left_high, left_low, right):
        right_high, right_low = split(right)
        return mm(left_high, right_high) + (mm(left_low, right_high) + mm(left_high, right_low))

    def put(index, value):
        start = pl.multiple_of(places_ref[1 + index] * width, width)
        out_ref[:, pl.ds(start, width)] = value

    first = jnp.concatenate([pieces[0][...], pieces[1][...]], axis=1)
    result = product(high, low, first)
    put(0, result[:, :width])
    put(1, result[:, width:])
    corner = jnp.concatenate([pieces[3][...], pieces[4][...]], axis=0)
    second = jnp.concatenate([pieces[2][...], corner], axis=1)
    result = product(high, low, second)
    put(2, result[:, :width])
    put(3, result[:, width:])


def plain_kernel(high_ref, low_ref, w_ref, o_ref):
    right_high, right_low = split(w_ref[...])
    high = high_ref[...]
    o_ref[...] = mm(high, right_high) + (mm(low_ref[...], right_high) + mm(high, right_low))


def from_partner(value, mask):
    pairs = [(source, source ^ mask) for source in range(lax.axis_size("seq"))]
    return lax.ppermute(value, "seq", pairs)


def local(queries, keys, values, log_decay, level_weights, norm_gain, out_weight):
    head_count, tok_count = log_decay.shape
    feature_count = queries.shape[1]
    size = feature_count // head_count
    tok_bits = tok_count.bit_length() - 1
    seq_size = lax.axis_size("seq")
    seq_bits = seq_size.bit_length() - 1
    seq_index = lax.axis_index("seq")
    head_size, head_index = lax.axis_size("head"), lax.axis_index("head")
    width = out_weight.shape[1]
    spread = width % LANES == 0 and seq_bits >= 2

    groups = []
    if spread:
        half = feature_count // 2
        for step in range(seq_size // 4):
            own = out_weight if step == 0 else from_partner(out_weight, 4 * step)
            groups.append([own])
        for step, group in enumerate(groups):
            own = group[0]
            by_x, by_y = from_partner(own, 1), from_partner(own, 2)
            low_rows, high_rows = by_x[:half], by_y[half:]
            corner_low = from_partner(low_rows, 2)
            corner_high = from_partner(high_rows, 1)
            group += [by_x, by_y, corner_low, corner_high]

    decay_sum = jnp.cumsum(log_decay, axis=1)
    decay_rows = decay_sum[:, None, :]
    tok_spec = pl.BlockSpec((tok_count, size), lambda h: (0, h))
    row_spec = pl.BlockSpec((1, 1, tok_count), lambda h: (h, 0, 0))
    state_spec = pl.BlockSpec((1, size + PAD_ROWS, size), lambda h: (h, 0, 0))
    out_spec = pl.BlockSpec((1, size, tok_count), lambda h: (h, 0, 0))
    state_flops = 6 * feature_count * tok_count * size
    call_state = pl.pallas_call(
        state_kernel,
        grid=(head_count,),
        in_specs=[tok_spec, tok_spec, row_spec],
        out_specs=state_spec,
        out_shape=jax.ShapeDtypeStruct((head_count, size + PAD_ROWS, size), jnp.float32),
        compiler_params=params(),
        cost_estimate=pl.CostEstimate(
            flops=state_flops,
            bytes_accessed=2 * keys.size * 4,
            transcendentals=head_count * tok_count,
        ),
        name="own_state",
    )
    own_state = call_state(keys, values, decay_rows)

    near_levels = level_weights[:, : tok_bits + 1, :]
    base_bits = min(LANES.bit_length() - 1, tok_bits)
    call_near = pl.pallas_call(
        functools.partial(near_kernel, base_bits, tok_bits),
        grid=(head_count,),
        in_specs=[
            tok_spec,
            tok_spec,
            tok_spec,
            row_spec,
            pl.BlockSpec((1, tok_bits + 1, tok_count), lambda h: (h, 0, 0)),
        ],
        out_specs=out_spec,
        out_shape=jax.ShapeDtypeStruct((head_count, size, tok_count), jnp.float32),
        compiler_params=params(),
        cost_estimate=pl.CostEstimate(
            flops=16 * state_flops,
            bytes_accessed=4 * keys.size * 4,
            transcendentals=head_count * tok_count * LANES,
        ),
        name="near",
    )
    near = call_near(queries, keys, values, decay_rows, near_levels)

    block = own_state
    inside = jnp.zeros((head_count,), jnp.float32)
    states, reaches = [], []
    for level_bit in range(seq_bits):
        other = from_partner(block, 2**level_bit)
        is_upper = seq_index >> level_bit & 1 == 1
        states.append(other)
        reaches.append(jnp.where(is_upper, jnp.exp(inside), 0.0))
        other_decay = other[:, size, 0]
        inside = jnp.where(is_upper, inside + other_decay, inside)
        if level_bit < seq_bits - 1:
            mine_decay = block[:, size:, :]
            decay_other = other[:, size:, :]
            late = jnp.where(is_upper, mine_decay, decay_other)[:, :1, :]
            low = jnp.where(is_upper, other, block)[:, :size, :]
            high = jnp.where(is_upper, block, other)[:, :size, :]
            merged = jnp.exp(late) * low + high
            block = jnp.concatenate([merged, mine_decay + decay_other], axis=1)
    far_levels = level_weights[:, tok_bits + 1 :, :]
    fade = jnp.exp(decay_sum)[:, None, :]

    def far_rows(first, last):
        reach = jnp.stack(reaches[first:last], axis=1)[:, :, None]
        return far_levels[:, first:last, :] * fade * reach

    def weight_spec(count):
        return pl.BlockSpec((1, count, tok_count), lambda h: (h, 0, 0))

    last = seq_bits - 1
    call_early = pl.pallas_call(
        early_kernel,
        grid=(head_count,),
        in_specs=[tok_spec, out_spec, weight_spec(last)] + [state_spec] * last,
        out_specs=out_spec,
        out_shape=jax.ShapeDtypeStruct((head_count, size, tok_count), jnp.float32),
        compiler_params=params(),
        cost_estimate=pl.CostEstimate(
            flops=last * state_flops, bytes_accessed=3 * keys.size * 4, transcendentals=0
        ),
        name="early",
    )
    early = call_early(queries, near, far_rows(0, last), *states[:last])
    call_far = pl.pallas_call(
        far_kernel,
        grid=(head_count,),
        in_specs=[tok_spec, out_spec, weight_spec(1), pl.BlockSpec((1, size), lambda h: (0, h))]
        + [state_spec],
        out_specs=[tok_spec, tok_spec],
        out_shape=[jax.ShapeDtypeStruct((tok_count, feature_count), jnp.bfloat16)] * 2,
        compiler_params=params(),
        cost_estimate=pl.CostEstimate(
            flops=state_flops, bytes_accessed=3 * keys.size * 4, transcendentals=0
        ),
        name="far",
    )
    normed_high, normed_low = call_far(
        queries, early, far_rows(last, seq_bits), norm_gain[None, :], states[last]
    )

    column_count = width * seq_size
    partial_shape = jax.ShapeDtypeStruct((tok_count, column_count), jnp.float32)
    whole = pl.BlockSpec(memory_space=pltpu.VMEM)
    if spread:
        partials = None
        low_bits = seq_index & 3
        for step, group in enumerate(groups):
            places = jnp.stack([(seq_index >> 2) ^ step] + [low_bits ^ e for e in range(4)])
            full = lambda rows, columns: pl.BlockSpec((rows, columns), lambda i, p: (0, 0))
            carried = [] if partials is None else [partials]
            partials = pl.pallas_call(
                project_kernel,
                grid_spec=pltpu.PrefetchScalarGridSpec(
                    num_scalar_prefetch=1,
                    grid=(1,),
                    in_specs=[full(tok_count, feature_count)] * 2
                    + [full(*piece.shape) for piece in group]
                    + [pl.BlockSpec(memory_space=pl.ANY)] * len(carried),
                    out_specs=pl.BlockSpec((tok_count, 4 * width), lambda i, p: (0, p[0])),
                ),
                out_shape=partial_shape,
                input_output_aliases={8: 0} if carried else {},
                compiler_params=params(),
                cost_estimate=pl.CostEstimate(
                    flops=6 * tok_count * feature_count * 4 * width,
                    bytes_accessed=4 * (feature_count * 4 * width + 2 * tok_count * feature_count),
                    transcendentals=0,
                ),
                name="project",
            )(places.astype(jnp.int32), normed_high, normed_low, *group, *carried)
    else:
        gathered = lax.all_gather(out_weight, "seq", axis=1, tiled=True)
        step = min(4 * LANES, column_count)
        partials = pl.pallas_call(
            plain_kernel,
            grid=(column_count // step,),
            in_specs=[
                pl.BlockSpec((tok_count, feature_count), lambda i: (0, 0)),
                pl.BlockSpec((tok_count, feature_count), lambda i: (0, 0)),
                pl.BlockSpec((feature_count, step), lambda i: (0, i)),
            ],
            out_specs=pl.BlockSpec((tok_count, step), lambda i: (0, i)),
            out_shape=partial_shape,
            compiler_params=params(),
            name="project",
        )(normed_high, normed_low, gathered)
    if head_size != 2:
        return lax.psum_scatter(partials, "head", scatter_dimension=1, tiled=True)
    share = column_count // 2
    sent = lax.dynamic_slice(partials, (0, (1 - head_index) * share), (tok_count, share))
    kept = lax.dynamic_slice(partials, (0, head_index * share), (tok_count, share))
    return kept + lax.ppermute(sent, "head", [(0, 1), (1, 0)])


def solution(mesh):
    return jax.shard_map(
        local,
        mesh=mesh,
        in_specs=(
            P("seq", "head"),
            P("seq", "head"),
            P("seq", "head"),
            P("head", "seq"),
            P("head", None, "seq"),
            P("head"),
            P("head", "seq"),
        ),
        out_specs=P("seq", "head"),
        check_vma=False,
    )
```
